256 devices in a mesh: group: 32 (over x, y, core), tp: 8 (over z).
Axes of the slice: x: 4, y: 4, z: 8, core: 2. Of those that a mesh axis runs over, the one named last changes fastest.
Arguments:
- hidden_in: bfloat16 [64, 3072], P('group'), may hold values from -6 to 6
- w_qkv: bfloat16 [3072, 2048], P(None, 'tp'), may hold values from -0.109375 to 0.109375
- w_out: bfloat16 [1536, 3072], P('tp'), may hold values from -0.15625 to 0.15625
- kv_pool: bfloat16 [2048, 128, 512], P(('group', 'tp'))
- page_table: int32 [64, 32], replicated, may hold values from 0 to 2047, as said below
- lengths: int32 [64], replicated, may hold values from 1 to 4096, as said below
Outputs:
- attn_proj: bfloat16 [64, 3072], P('group', 'tp')
The draws below stay inside these ranges and needn't reach their ends.
Inputs may be any that keep to these rules, and one draw needn't show every extreme that they name: `page_table`: every pool slot is named by exactly one request page. `lengths`: some request has the full 32 * 128 cached tokens.
All inputs are finite; a program needn't handle non-finite values.
Results may differ from the reference program's by a relative error of at most 0.0085.
The reference program's roundings to bfloat16 on the way count: a program that leaves them out, or rounds other values in their place, can miss the bound.
Values may be sent and summed in bfloat16 or wider, within the bound.
A program may use at most 64 MiB of HBM per device.

```python
import jax
import jax.numpy as jnp
from jax import lax

D = 3072
HEADS = 12
KV_HEADS = 2
HEAD_DIM = 128
PAGE = 128
MAX_PAGES = 32
REQUESTS = 64
SLOTS = 2048


def draw_kv_pool(key, part):
    width = 2 * KV_HEADS * HEAD_DIM
    base = jax.random.normal(jax.random.fold_in(key, 1), (SLOTS, PAGE, width), jnp.float32)
    return base.astype(jnp.bfloat16)


def draw_page_table(key, part):
    order = jax.random.permutation(jax.random.fold_in(key, 3), SLOTS)
    return order.astype(jnp.int32).reshape(REQUESTS, MAX_PAGES)


def draw_lengths(key, part):
    drawn = jax.random.randint(jax.random.fold_in(key, 4), (REQUESTS,), 1, MAX_PAGES * PAGE + 1).astype(jnp.int32)
    return drawn.at[0].set(MAX_PAGES * PAGE)


def levels(own_key, shape, cuts, low, largest):
    def one(position, parts):
        draws = jax.random.uniform(jax.random.fold_in(jax.random.fold_in(own_key, 6), position), (parts,), jnp.float32, low / len(cuts), largest / len(cuts))
        return jnp.repeat(jnp.exp(draws), shape[position] // parts).reshape((-1,) + (1,) * (len(shape) - position - 1))

    loudness = one(*cuts[0])
    for cut in cuts[1:]:
        loudness = loudness * one(*cut)
    return loudness


def centred(stream_key, extent, scale, most, split=(), held_as=jnp.bfloat16):
    level = levels(stream_key, extent, split, -0.22, 0.18) if split else 1.0
    array = jax.random.normal(stream_key, extent, jnp.float32) * scale * level
    return jnp.minimum(jnp.maximum(array, -most), most).astype(held_as)


def setup_inputs(seed: int = 0) -> dict:
    arg_keys = jax.random.split(jax.random.key(seed), 7)
    hidden_in = centred(arg_keys[0], (REQUESTS, D), 1.0, 6.0, ((0, 32),))
    w_qkv = centred(arg_keys[1], (D, (HEADS + 2 * KV_HEADS) * HEAD_DIM), D ** -0.5, 0.109375, ((1, 8),))
    w_out = centred(arg_keys[2], (HEADS * HEAD_DIM, D), (HEADS * HEAD_DIM) ** -0.5, 0.15625, ((0, 8),))
    kv_pool = draw_kv_pool(jax.random.fold_in(arg_keys[6], 71), 0)
    page_table = draw_page_table(jax.random.fold_in(arg_keys[6], 71), 0)
    lengths = draw_lengths(jax.random.fold_in(arg_keys[6], 71), 0)
    return {"hidden_in": hidden_in, "w_qkv": w_qkv, "w_out": w_out, "kv_pool": kv_pool, "page_table": page_table, "lengths": lengths}


def reference(hidden_in, w_qkv, w_out, kv_pool, page_table, lengths):
    qdim = HEADS * HEAD_DIM
    kdim = KV_HEADS * HEAD_DIM
    per_kv = HEADS // KV_HEADS
    scale = HEAD_DIM ** -0.5
    qkv = jnp.dot(hidden_in, w_qkv, preferred_element_type=jnp.float32).astype(jnp.bfloat16)
    queries = qkv[:, :qdim].reshape(REQUESTS, KV_HEADS, per_kv, HEAD_DIM)
    new_keys = qkv[:, qdim:qdim + kdim].reshape(REQUESTS, KV_HEADS, HEAD_DIM)
    new_values = qkv[:, qdim + kdim:].reshape(REQUESTS, KV_HEADS, HEAD_DIM)
    positions = jnp.arange(MAX_PAGES)[:, None] * PAGE + jnp.arange(PAGE)[None, :]

    def one_request(items):
        query, pages, length = items
        cache = kv_pool[pages]
        keys = cache[..., :kdim].reshape(MAX_PAGES, PAGE, KV_HEADS, HEAD_DIM).astype(jnp.float32)
        values = cache[..., kdim:].reshape(MAX_PAGES, PAGE, KV_HEADS, HEAD_DIM).astype(jnp.float32)
        scores = jnp.einsum("gjd,ptgd->pgjt", query.astype(jnp.float32), keys) * scale
        live = (positions < length)[:, None, None, :]
        top = jnp.max(jnp.where(live, scores, -1e30), axis=-1)
        probs = jnp.where(live, jnp.exp(scores - top[..., None]), 0.0).astype(jnp.bfloat16).astype(jnp.float32)
        total = jnp.sum(probs, axis=-1)
        weighted = jnp.einsum("pgjt,ptgd->pgjd", probs, values)
        best = jnp.max(top, axis=0)
        factor = jnp.exp(top - best[None])
        return best, jnp.sum(total * factor, axis=0), jnp.sum(weighted * factor[..., None], axis=0)

    best, total, weighted = lax.map(one_request, (queries, page_table, lengths))
    own = jnp.einsum("rgjd,rgd->rgj", queries.astype(jnp.float32), new_keys.astype(jnp.float32)) * scale
    peak = jnp.maximum(best, own)
    old_factor = jnp.exp(best - peak)
    own_factor = jnp.exp(own - peak)
    total = total * old_factor + own_factor
    weighted = weighted * old_factor[..., None] + own_factor[..., None] * new_values.astype(jnp.float32)[:, :, None, :]
    attn = (weighted / total[..., None]).reshape(REQUESTS, qdim).astype(jnp.bfloat16)
    return jnp.dot(attn, w_out, preferred_element_type=jnp.float32).astype(jnp.bfloat16)
```

```python
import functools

import jax
import jax.numpy as jnp
from jax import lax
from jax.experimental import pallas as pl
from jax.experimental.pallas import tpu as pltpu
from jax.sharding import PartitionSpec as P

HEADS = 12
KV_HEADS = 2
HEAD_DIM = 128
PER_KV = HEADS // KV_HEADS
NEG = -1e30
MESH = pl.DeviceIdType.MESH
F32 = jnp.float32
BF16 = jnp.bfloat16


def iota(shape, dim):
    return lax.broadcasted_iota(jnp.int32, shape, dim)


def kernel(
    G, T,
    hid_ref, wq_hbm, wo_hbm, kv_hbm, pt_ref, len_ref, out_ref,
    wq, wo, kv, qsend, qall, qown, bsend, brecv, dsend, drecv, esend, erecv, psend, precv,
    local_sem,
    qs_sem, qr_sem, os_sem, or_sem, bs_sem, br_sem, ds_sem, dr_sem, es_sem, er_sem, ps_sem, pr_sem,
):
    me_g = lax.axis_index("group")
    me_t = lax.axis_index("tp")
    scale = HEAD_DIM ** (-0.5)
    S = kv_hbm.shape[0]
    page_len = kv_hbm.shape[1]
    R = pt_ref.shape[0]
    max_pages = pt_ref.shape[1]
    ring = S * T
    par = lax.rem(me_t, 2)
    hd = HEAD_DIM

    wo_rows = wo_hbm.shape[0]
    wo_base = pl.multiple_of(par * 64, 64)
    cp_wq = pltpu.make_async_copy(wq_hbm, wq, local_sem.at[0])
    cp_kv = pltpu.make_async_copy(kv_hbm, kv, local_sem.at[1])
    cp_wo = pltpu.make_async_copy(wo_hbm, wo.at[pl.ds(wo_base, wo_rows)], local_sem.at[2])
    cp_wq.start()
    cp_kv.start()
    cp_wo.start()

    barrier = pltpu.get_barrier_semaphore()

    def greet_g(d, c):
        pl.semaphore_signal(barrier, inc=1, device_id=(lax.rem(me_g + d, G), me_t), device_id_type=MESH)
        return c

    def greet_t(d, c):
        pl.semaphore_signal(barrier, inc=1, device_id=(me_g, lax.rem(me_t + d, T)), device_id_type=MESH)
        return c

    lax.fori_loop(1, G, greet_g, 0)
    lax.fori_loop(1, T, greet_t, 0)

    zero_base = pl.multiple_of((1 - par) * wo_rows, 64)
    wo[pl.ds(zero_base, 64), :] = jnp.zeros((64, wo.shape[1]), BF16)

    cp_wq.wait()
    qkv = jnp.dot(hid_ref[...], wq[...], preferred_element_type=F32).astype(BF16)
    qsend[...] = qkv
    qall[me_g] = qkv
    qown[me_t] = qkv

    pl.semaphore_wait(barrier, G - 1 + T - 1)

    def to_g(src, dst, ssem, rsem, d, chunked):
        peer = lax.rem(me_g + d, G)
        return pltpu.make_async_remote_copy(
            src_ref=src.at[peer] if chunked else src,
            dst_ref=dst.at[me_g],
            send_sem=ssem.at[d],
            recv_sem=rsem.at[d],
            device_id=(peer, me_t),
            device_id_type=MESH,
        )

    def to_t(src, dst, ssem, rsem, d, chunked):
        peer = lax.rem(me_t + d, T)
        return pltpu.make_async_remote_copy(
            src_ref=src.at[peer] if chunked else src,
            dst_ref=dst.at[me_t],
            send_sem=ssem.at[d],
            recv_sem=rsem.at[d],
            device_id=(me_g, peer),
            device_id_type=MESH,
        )

    def each(n, copy, what):
        def body(d, c):
            getattr(copy(d), what)()
            return c

        lax.fori_loop(1, n, body, 0)

    q_copy = lambda d: to_g(qsend, qall, qs_sem, qr_sem, d, False)
    o_copy = lambda d: to_t(qsend, qown, os_sem, or_sem, d, False)
    b_copy = lambda d: to_t(bsend, brecv, bs_sem, br_sem, d, True)
    d_copy = lambda d: to_t(dsend, drecv, ds_sem, dr_sem, d, True)
    e_copy = lambda d: to_g(esend, erecv, es_sem, er_sem, d, True)
    p_copy = lambda d: to_t(psend, precv, ps_sem, pr_sem, d, True)

    each(G, q_copy, "start")
    each(T, o_copy, "start")

    slot = me_g * ring + iota((R, ring), 1)
    table = pt_ref[...]
    length_row = len_ref[...]
    length_col = jnp.sum(
        jnp.where(iota((R, R), 0) == iota((R, R), 1), jnp.broadcast_to(length_row, (R, R)), 0),
        axis=1, keepdims=True,
    )
    marks = jnp.zeros((R, ring), jnp.int32)
    for j in range(max_pages):
        marks = jnp.where(table[:, j : j + 1] == slot, j + 1, marks)
    owns = marks > 0
    live_row = jnp.sum(
        jnp.where(owns, length_col - (marks - 1) * page_len, 0), axis=0, keepdims=True
    )
    mine = iota((S, ring), 1) == me_t * S + iota((S, ring), 0)
    live_col = jnp.sum(
        jnp.where(mine, jnp.broadcast_to(live_row, (S, ring)), 0), axis=1, keepdims=True
    )
    live8 = iota((S, page_len), 1) < live_col
    live = jnp.concatenate([live8.astype(F32)] * PER_KV, axis=0) > 0.5
    owns_b = owns.astype(F32).astype(BF16)

    each(G, q_copy, "wait_recv")
    q_rows = jnp.concatenate([qall[g] for g in range(G)], axis=0)
    chosen = lax.dot_general(
        owns_b, q_rows, (((0,), (0,)), ((), ())), preferred_element_type=F32
    )
    for t in range(T):
        bsend[t] = chosen[t * S : (t + 1) * S, :].astype(BF16)
    brecv[me_t] = bsend[me_t]
    each(T, b_copy, "start")

    cp_kv.wait()
    each(T, b_copy, "wait_recv")

    rows = PER_KV * S
    row_slot = lax.rem(iota((rows, page_len), 0), S)
    tops, totals, sums = [], [], []
    for g in range(KV_HEADS):
        pieces = []
        for j in range(PER_KV):
            h = g * PER_KV + j
            pieces.append(brecv[h // 2].astype(F32)[:, (h % 2) * hd : (h % 2 + 1) * hd])
        q = jnp.concatenate(pieces, axis=0).astype(BF16)
        scores = jnp.zeros((rows, page_len), F32)
        for s in range(S):
            key = kv[s, :, g * hd : (g + 1) * hd]
            part = lax.dot_general(q, key, (((1,), (1,)), ((), ())), preferred_element_type=F32)
            scores = jnp.where(row_slot == s, part, scores)
        scores = scores * scale
        top = jnp.max(jnp.where(live, scores, NEG), axis=1, keepdims=True)
        prob = jnp.where(live, jnp.exp(scores - top), 0.0).astype(BF16)
        total = jnp.sum(prob.astype(F32), axis=1, keepdims=True)
        acc = jnp.zeros((rows, hd), F32)
        for s in range(S):
            value = kv[s, :, (KV_HEADS + g) * hd : (KV_HEADS + g + 1) * hd]
            part = jnp.dot(prob, value, preferred_element_type=F32)
            acc = jnp.where(row_slot == s, part, acc)
        for j in range(PER_KV):
            cut = slice(j * S, (j + 1) * S)
            tops.append(top[cut])
            totals.append(total[cut])
            sums.append(acc[cut])

    lane8 = iota((S, hd), 1)
    for t in range(T):
        h = (3 * t) // 2
        dsend[t, :, 0:hd] = sums[h]
        dsend[t, :, hd : 2 * hd] = sums[h + 1]
        dsend[t, :, 2 * hd : 3 * hd] = jnp.where(
            lane8 == 0, tops[h],
            jnp.where(lane8 == 1, tops[h + 1], jnp.where(lane8 == 2, totals[h], totals[h + 1])),
        )
    drecv[me_t] = dsend[me_t]
    each(T, d_copy, "start")
    each(T, d_copy, "wait_recv")

    got = drecv[...].reshape(ring, 3 * hd)
    stats = got[:, 2 * hd : 3 * hd]
    same = iota((ring, ring), 0) == iota((ring, ring), 1)
    peaks, wholes, outs = [], [], []
    for i in range(2):
        m_row = jnp.sum(jnp.where(same, stats[:, i : i + 1], 0.0), axis=0, keepdims=True)
        m_all = jnp.where(owns, jnp.broadcast_to(m_row, (R, ring)), NEG)
        peak = jnp.max(m_all, axis=1, keepdims=True)
        weight = jnp.exp(jnp.where(owns, m_row - peak, NEG))
        both = jnp.concatenate([got[:, i * hd : (i + 1) * hd], stats], axis=1)
        mixed = jnp.dot(
            weight, both, preferred_element_type=F32, precision=lax.Precision.HIGHEST
        )
        peaks.append(peak)
        wholes.append(mixed[:, hd + 2 + i : hd + 3 + i])
        outs.append(mixed[:, :hd])
    lane_r = iota((R, hd), 1)
    mixed_stats = jnp.where(
        lane_r == 0, peaks[0],
        jnp.where(lane_r == 1, peaks[1], jnp.where(lane_r == 2, wholes[0], wholes[1])),
    )
    packed = jnp.concatenate([outs[0], outs[1], mixed_stats], axis=1)
    per = R // G
    for g in range(G):
        esend[g] = packed[g * per : (g + 1) * per, :]
    erecv[me_g] = esend[me_g]
    each(G, e_copy, "start")

    each(T, o_copy, "wait_recv")
    first = lax.div(3 * me_t, 2)

    def own_head(h):
        pair = qown[lax.div(h, 2)].astype(F32)
        return jnp.where(lax.rem(h, 2) == 0, pair[:, :hd], pair[:, hd:])

    def own_kv(row, h):
        pair = qown[row].astype(F32)
        return jnp.where(lax.div(h, PER_KV) == 0, pair[:, :hd], pair[:, hd:])

    own_scores = [
        jnp.sum(own_head(first + i) * own_kv(6, first + i), axis=1, keepdims=True) * scale
        for i in range(2)
    ]
    own_values = [own_kv(7, first + i) for i in range(2)]
    cp_wo.wait()
    each(G, e_copy, "wait_recv")

    every = erecv[...]
    heads = []
    for i in range(2):
        m = every[:, :, 2 * hd + i : 2 * hd + i + 1]
        l = every[:, :, 2 * hd + 2 + i : 2 * hd + 3 + i]
        peak = jnp.maximum(jnp.max(m, axis=0), own_scores[i])
        f = jnp.exp(m - peak[None])
        own_f = jnp.exp(own_scores[i] - peak)
        whole = jnp.sum(f * l, axis=0) + own_f
        summed = jnp.sum(f * every[:, :, i * hd : (i + 1) * hd], axis=0) + own_f * own_values[i]
        heads.append(summed / whole)
    attn = jnp.concatenate(heads, axis=1)
    col = iota(attn.shape, 1)
    attn = jnp.where((col >= par * 64) & (col < par * 64 + wo_rows), attn, 0.0).astype(BF16)
    part = jnp.dot(attn, wo[...], preferred_element_type=F32)
    width = out_ref.shape[1]
    for t in range(T):
        psend[t] = part[:, t * width : (t + 1) * width]
    precv[me_t] = psend[me_t]
    each(T, p_copy, "start")
    each(T, p_copy, "wait_recv")
    out_ref[...] = jnp.sum(precv[...], axis=0).astype(BF16)

    each(G, q_copy, "wait_send")
    each(T, o_copy, "wait_send")
    each(T, b_copy, "wait_send")
    each(T, d_copy, "wait_send")
    each(G, e_copy, "wait_send")
    each(T, p_copy, "wait_send")


def solution(mesh):
    G, T = mesh.shape["group"], mesh.shape["tp"]

    def on_device(hidden_in, w_qkv, w_out, kv_pool, page_table, lengths):
        per = hidden_in.shape[0]
        cols = w_qkv.shape[1]
        slots = kv_pool.shape[0]
        depth = w_out.shape[1]
        width = depth // T
        wide = 3 * HEAD_DIM
        dma = pltpu.SemaphoreType.DMA
        vm = pl.BlockSpec(memory_space=pltpu.VMEM)
        hbm = pl.BlockSpec(memory_space=pl.ANY)
        return pl.pallas_call(
            functools.partial(kernel, G, T),
            name="decode",
            out_shape=jax.ShapeDtypeStruct((per, width), BF16),
            in_specs=[vm, hbm, hbm, hbm, vm, vm],
            out_specs=vm,
            scratch_shapes=[
                pltpu.VMEM(w_qkv.shape, BF16),
                pltpu.VMEM((2 * HEAD_DIM, depth), BF16),
                pltpu.VMEM(kv_pool.shape, BF16),
                pltpu.VMEM((per, cols), BF16),
                pltpu.VMEM((G, per, cols), BF16),
                pltpu.VMEM((T, per, cols), BF16),
                pltpu.VMEM((T, slots, cols), BF16),
                pltpu.VMEM((T, slots, cols), BF16),
                pltpu.VMEM((T, slots, wide), F32),
                pltpu.VMEM((T, slots, wide), F32),
                pltpu.VMEM((G, per, wide), F32),
                pltpu.VMEM((G, per, wide), F32),
                pltpu.VMEM((T, per, width), F32),
                pltpu.VMEM((T, per, width), F32),
                dma((3,)),
                dma((G,)), dma((G,)), dma((T,)), dma((T,)), dma((T,)), dma((T,)),
                dma((T,)), dma((T,)), dma((G,)), dma((G,)), dma((T,)), dma((T,)),
            ],
            compiler_params=pltpu.CompilerParams(collective_id=0, has_side_effects=True),
        )(hidden_in, w_qkv, w_out, kv_pool, page_table, lengths.reshape(1, -1))

    return jax.shard_map(
        on_device,
        mesh=mesh,
        in_specs=(
            P("group", None),
            P(None, "tp"),
            P("tp", None),
            P(("group", "tp"), None, None),
            P(),
            P(),
        ),
        out_specs=P("group", "tp"),
        check_vma=False,
    )
```

```python
import functools

import jax
import jax.numpy as jnp
from jax import lax
from jax.experimental import pallas as pl
from jax.experimental.pallas import tpu as pltpu
from jax.sharding import PartitionSpec as P

HEADS = 12
KV_HEADS = 2
HEAD_DIM = 128
PER_KV = HEADS // KV_HEADS
NEG = -1e30
MESH = pl.DeviceIdType.MESH
F32 = jnp.float32
BF16 = jnp.bfloat16


def iota(shape, dim):
    return lax.broadcasted_iota(jnp.int32, shape, dim)


def pieces3(x):
    hi = x.astype(BF16).astype(F32)
    mid = (x - hi).astype(BF16).astype(F32)
    return [hi, mid, x - hi - mid]


def order_t(T):
    return sorted(range(1, T), key=lambda d: -min(d, T - d))


def order_g(n):
    hops = lambda d: min(d, n - d)
    all_d = [(x, y, c) for x in range(n) for y in range(n) for c in range(2)]
    return sorted(all_d[1:], key=lambda o: -(hops(o[0]) + hops(o[1])) * 2 - o[2])


def spread(columns, lane, width):
    out = columns[-1]
    for i in range(len(columns) - 2, -1, -1):
        out = jnp.where(lane == i, columns[i], out)
    return jnp.broadcast_to(out, (out.shape[0], width))


def kernel(
    G, T,
    hid_hbm, wq_hbm, wo_hbm, kv_hbm, pt_hbm, len_hbm, out_ref,
    hid, pt, lens, wq, wo, kv,
    qsend, qall, qown, bsend, brecv, dsend, drecv, esend, erecv, psend, precv,
    local_sem, send_sem, recv_sem,
):
    me_g = lax.axis_index("group")
    me_t = lax.axis_index("tp")
    scale = HEAD_DIM ** (-0.5)
    S = kv_hbm.shape[0]
    page_len = kv_hbm.shape[1]
    max_pages, R = pt_hbm.shape
    ring = S * T
    par = lax.rem(me_t, 2)
    hd = HEAD_DIM
    side = 1
    while 2 * side * side < G:
        side += 1

    xs = [lax.rem(lax.div(me_g, 2 * side) + d, side) * (2 * side) for d in range(side)]
    ys = [lax.rem(lax.rem(lax.div(me_g, 2), side) + d, side) * 2 for d in range(side)]
    cs = [lax.rem(lax.rem(me_g, 2) + d, 2) for d in range(2)]
    peers_g = [xs[dx] + ys[dy] + cs[dc] for dx, dy, dc in order_g(side)]
    peers_t = [lax.rem(me_t + d, T) for d in order_t(T)]

    barrier = pltpu.get_barrier_semaphore()
    for p in peers_t:
        pl.semaphore_signal(barrier, inc=1, device_id=(me_g, p), device_id_type=MESH)
    for p in peers_g:
        pl.semaphore_signal(barrier, inc=1, device_id=(p, me_t), device_id_type=MESH)

    wo_rows = wo_hbm.shape[0]
    wo_base = pl.multiple_of(par * 64, 64)
    loads = [
        pltpu.make_async_copy(src, dst, local_sem.at[i])
        for i, (src, dst) in enumerate([
            (hid_hbm, hid), (wq_hbm, wq), (pt_hbm, pt), (len_hbm, lens), (kv_hbm, kv),
            (wo_hbm, wo.at[pl.ds(wo_base, wo_rows)]),
        ])
    ]
    for load in loads:
        load.start()
    cp_hid, cp_wq, cp_pt, cp_len, cp_kv, cp_wo = loads

    zero_base = pl.multiple_of((1 - par) * wo_rows, 64)
    wo[pl.ds(zero_base, 64), :] = jnp.zeros((64, wo.shape[1]), BF16)

    cp_hid.wait()
    cp_wq.wait()
    qkv = jnp.dot(hid[...], wq[...], preferred_element_type=F32).astype(BF16)
    qsend[...] = qkv
    qall[me_g] = qkv
    qown[me_t] = qkv

    def send_g(k, src, dst, chunked):
        for p in peers_g:
            pltpu.make_async_remote_copy(
                src_ref=src.at[p] if chunked else src, dst_ref=dst.at[me_g],
                send_sem=send_sem.at[k], recv_sem=recv_sem.at[k],
                device_id=(p, me_t), device_id_type=MESH,
            ).start()

    def send_t(k, src, dst, chunked):
        for p in peers_t:
            pltpu.make_async_remote_copy(
                src_ref=src.at[p] if chunked else src, dst_ref=dst.at[me_t],
                send_sem=send_sem.at[k], recv_sem=recv_sem.at[k],
                device_id=(me_g, p), device_id_type=MESH,
            ).start()

    def wait(sems, k, dst):
        most = dst.at[pl.ds(0, dst.shape[0] - 1)]
        pltpu.make_async_copy(most, most, sems.at[k]).wait()

    pl.semaphore_wait(barrier, G - 1 + T - 1)
    send_g(0, qsend, qall, False)
    send_t(1, qsend, qown, False)

    cp_pt.wait()
    cp_len.wait()

    def find(first, count):
        slot = first + iota((count, R), 0)
        marks = jnp.zeros((count, R), jnp.int32)
        for j in range(max_pages):
            marks = jnp.where(pt[j : j + 1, :] == slot, j + 1, marks)
        return marks

    held = (find(me_g * ring, ring) > 0).astype(F32).astype(BF16)
    eye = (iota((R, R), 0) == iota((R, R), 1)).astype(F32).astype(BF16)
    owns = lax.dot_general(
        eye, held, (((1,), (1,)), ((), ())), preferred_element_type=F32
    ) > 0.5
    marks = find(me_g * ring + me_t * S, S)
    live_col = jnp.sum(
        jnp.where(marks > 0, lens[...] - (marks - 1) * page_len, 0), axis=1, keepdims=True
    )
    live8 = iota((S, page_len), 1) < live_col
    live = jnp.concatenate([live8.astype(F32)] * PER_KV, axis=0) > 0.5

    wait(recv_sem, 0, qall)
    q_rows = jnp.concatenate([qall[g] for g in range(G)], axis=0)
    chosen = jnp.dot(held, q_rows, preferred_element_type=F32)
    for t in range(T):
        bsend[t] = chosen[t * S : (t + 1) * S, :].astype(BF16)
    brecv[me_t] = bsend[me_t]
    send_t(2, bsend, brecv, True)

    cp_kv.wait()
    wait(recv_sem, 2, brecv)

    rows = PER_KV * S
    row_slot = lax.rem(iota((rows, page_len), 0), S)
    tops, totals, sums = [], [], []
    for g in range(KV_HEADS):
        parts = []
        for j in range(PER_KV):
            h = g * PER_KV + j
            parts.append(brecv[h // 2].astype(F32)[:, (h % 2) * hd : (h % 2 + 1) * hd])
        q = jnp.concatenate(parts, axis=0).astype(BF16)
        scores = jnp.zeros((rows, page_len), F32)
        for s in range(S):
            key = kv[s, :, g * hd : (g + 1) * hd]
            part = lax.dot_general(q, key, (((1,), (1,)), ((), ())), preferred_element_type=F32)
            scores = jnp.where(row_slot == s, part, scores)
        scores = scores * scale
        top = jnp.max(jnp.where(live, scores, NEG), axis=1, keepdims=True)
        prob = jnp.where(live, jnp.exp(scores - top), 0.0).astype(BF16)
        total = jnp.sum(prob.astype(F32), axis=1, keepdims=True)
        acc = jnp.zeros((rows, hd), F32)
        for s in range(S):
            value = kv[s, :, (KV_HEADS + g) * hd : (KV_HEADS + g + 1) * hd]
            part = jnp.dot(prob, value, preferred_element_type=F32)
            acc = jnp.where(row_slot == s, part, acc)
        for j in range(PER_KV):
            cut = slice(j * S, (j + 1) * S)
            tops.append(pieces3(top[cut]))
            totals.append(pieces3(total[cut]))
            sums.append(acc[cut])

    lane8 = iota((S, hd), 1)
    for t in range(T):
        h = (3 * t) // 2
        stats = spread(tops[h] + tops[h + 1] + totals[h] + totals[h + 1], lane8, hd)
        dsend[t] = jnp.concatenate([sums[h], sums[h + 1], stats], axis=1).astype(BF16)
    drecv[me_t] = dsend[me_t]
    send_t(3, dsend, drecv, True)
    wait(recv_sem, 3, drecv)

    got = drecv[...].astype(F32).reshape(ring, 3 * hd)
    same = iota((ring, ring), 0) == iota((ring, ring), 1)
    peaks, weights = [], []
    for i in range(2):
        c = 2 * hd + 3 * i
        m_col = got[:, c : c + 1] + got[:, c + 1 : c + 2] + got[:, c + 2 : c + 3]
        m_row = jnp.sum(jnp.where(same, m_col, 0.0), axis=0, keepdims=True)
        peak = jnp.max(jnp.where(owns, m_row, NEG), axis=1, keepdims=True)
        weight = jnp.exp(jnp.where(owns, m_row - peak, NEG))
        peaks.append(peak)
        high = weight.astype(BF16).astype(F32)
        weights += [high, weight - high]
    mixed = jnp.dot(
        jnp.concatenate(weights, axis=0).astype(BF16), got.astype(BF16),
        preferred_element_type=F32,
    )
    wholes, outs = [], []
    for i in range(2):
        both = mixed[2 * i * R : (2 * i + 1) * R] + mixed[(2 * i + 1) * R : (2 * i + 2) * R]
        c = 2 * hd + 6 + 3 * i
        wholes.append(both[:, c : c + 1] + both[:, c + 1 : c + 2] + both[:, c + 2 : c + 3])
        outs.append(both[:, i * hd : (i + 1) * hd])
    mixed_stats = spread(peaks + wholes, iota((R, hd), 1), hd)
    packed = jnp.concatenate(outs + [mixed_stats], axis=1)
    per = R // G
    for g in range(G):
        esend[g] = packed[g * per : (g + 1) * per, :]
    erecv[me_g] = esend[me_g]
    send_g(4, esend, erecv, True)

    wait(recv_sem, 1, qown)
    first = lax.div(3 * me_t, 2)

    def own_head(h):
        pair = qown[lax.div(h, 2)].astype(F32)
        return jnp.where(lax.rem(h, 2) == 0, pair[:, :hd], pair[:, hd:])

    def own_kv(row, h):
        pair = qown[row].astype(F32)
        return jnp.where(lax.div(h, PER_KV) == 0, pair[:, :hd], pair[:, hd:])

    own_scores = [
        jnp.sum(own_head(first + i) * own_kv(6, first + i), axis=1, keepdims=True) * scale
        for i in range(2)
    ]
    own_values = [own_kv(7, first + i) for i in range(2)]
    cp_wo.wait()
    wait(recv_sem, 4, erecv)

    every = erecv[...]
    heads = []
    for i in range(2):
        m = every[:, :, 2 * hd + i : 2 * hd + i + 1]
        l = every[:, :, 2 * hd + 2 + i : 2 * hd + 3 + i]
        peak = jnp.maximum(jnp.max(m, axis=0), own_scores[i])
        f = jnp.exp(m - peak[None])
        own_f = jnp.exp(own_scores[i] - peak)
        whole = jnp.sum(f * l, axis=0) + own_f
        summed = jnp.sum(f * every[:, :, i * hd : (i + 1) * hd], axis=0) + own_f * own_values[i]
        heads.append(summed / whole)
    attn = jnp.concatenate(heads, axis=1)
    col = iota(attn.shape, 1)
    attn = jnp.where((col >= par * 64) & (col < par * 64 + wo_rows), attn, 0.0).astype(BF16)
    part = jnp.dot(attn, wo[...], preferred_element_type=F32)
    width = out_ref.shape[1]
    for t in range(T):
        psend[t] = part[:, t * width : (t + 1) * width]
    precv[me_t] = psend[me_t]
    send_t(5, psend, precv, True)
    wait(recv_sem, 5, precv)
    out_ref[...] = jnp.sum(precv[...], axis=0).astype(BF16)

    for k, dst in enumerate([qall, qown, brecv, drecv, erecv, precv]):
        wait(send_sem, k, dst)


def solution(mesh):
    G, T = mesh.shape["group"], mesh.shape["tp"]

    def on_device(hidden_in, w_qkv, w_out, kv_pool, page_table, lengths):
        per = hidden_in.shape[0]
        cols = w_qkv.shape[1]
        slots = kv_pool.shape[0]
        depth = w_out.shape[1]
        width = depth // T
        wide = 3 * HEAD_DIM
        dma = pltpu.SemaphoreType.DMA
        vm = pl.BlockSpec(memory_space=pltpu.VMEM)
        hbm = pl.BlockSpec(memory_space=pl.ANY)
        return pl.pallas_call(
            functools.partial(kernel, G, T),
            name="decode",
            out_shape=jax.ShapeDtypeStruct((per, width), BF16),
            in_specs=[hbm] * 6,
            out_specs=vm,
            scratch_shapes=[
                pltpu.VMEM(hidden_in.shape, BF16),
                pltpu.VMEM(page_table.shape[::-1], jnp.int32),
                pltpu.VMEM((1, lengths.shape[0]), jnp.int32),
                pltpu.VMEM(w_qkv.shape, BF16),
                pltpu.VMEM((2 * HEAD_DIM, depth), BF16),
                pltpu.VMEM(kv_pool.shape, BF16),
                pltpu.VMEM((per, cols), BF16),
                pltpu.VMEM((G, per, cols), BF16),
                pltpu.VMEM((T, per, cols), BF16),
                pltpu.VMEM((T, slots, cols), BF16),
                pltpu.VMEM((T, slots, cols), BF16),
                pltpu.VMEM((T, slots, wide), BF16),
                pltpu.VMEM((T, slots, wide), BF16),
                pltpu.VMEM((G, per, wide), F32),
                pltpu.VMEM((G, per, wide), F32),
                pltpu.VMEM((T, per, width), F32),
                pltpu.VMEM((T, per, width), F32),
                dma((6,)), dma((6,)), dma((6,)),
            ],
            compiler_params=pltpu.CompilerParams(collective_id=0, has_side_effects=True),
        )(hidden_in, w_qkv, w_out, kv_pool, page_table.T, lengths.reshape(1, -1))

    return jax.shard_map(
        on_device,
        mesh=mesh,
        in_specs=(
            P("group", None),
            P(None, "tp"),
            P("tp", None),
            P(("group", "tp"), None, None),
            P(),
            P(),
        ),
        out_specs=P("group", "tp"),
        check_vma=False,
    )
```

```python
import functools

import jax
import jax.numpy as jnp
from jax import lax
from jax.experimental import pallas as pl
from jax.experimental.pallas import tpu as pltpu
from jax.sharding import PartitionSpec as P

HEADS = 12
KV_HEADS = 2
HEAD_DIM = 128
PER_KV = HEADS // KV_HEADS
NEG = -1e30
MESH = pl.DeviceIdType.MESH
F32 = jnp.float32
BF16 = jnp.bfloat16


def iota(shape, dim):
    return lax.broadcasted_iota(jnp.int32, shape, dim)


def order_t(T):
    return sorted(range(1, T), key=lambda d: -min(d, T - d))


def order_g(n):
    hops = lambda d: min(d, n - d)
    all_d = [(x, y, c) for x in range(n) for y in range(n) for c in range(2)]
    return sorted(all_d[1:], key=lambda o: -(hops(o[0]) + hops(o[1])) * 2 - o[2])


def spread(columns, lane, width):
    out = columns[-1]
    for i in range(len(columns) - 2, -1, -1):
        out = jnp.where(lane == i, columns[i], out)
    return jnp.broadcast_to(out, (out.shape[0], width))


def kernel(
    G, T,
    hid_hbm, wq_hbm, wo_hbm, kv_hbm, pt_hbm, len_hbm, precv,
    hid, pt, lens, wq, wo, kv,
    qsend, qall, qown, bsend, brecv, dsend, drecv, esend, erecv, psend,
    local_sem, send_sem, recv_sem,
):
    me_g = lax.axis_index("group")
    me_t = lax.axis_index("tp")
    scale = HEAD_DIM ** (-0.5)
    S = kv_hbm.shape[0]
    page_len = kv_hbm.shape[1]
    max_pages, R = pt_hbm.shape
    ring = S * T
    par = lax.rem(me_t, 2)
    hd = HEAD_DIM
    side = 1
    while 2 * side * side < G:
        side += 1

    xs = [lax.rem(lax.div(me_g, 2 * side) + d, side) * (2 * side) for d in range(side)]
    ys = [lax.rem(lax.rem(lax.div(me_g, 2), side) + d, side) * 2 for d in range(side)]
    cs = [lax.rem(lax.rem(me_g, 2) + d, 2) for d in range(2)]
    peers_g = [xs[dx] + ys[dy] + cs[dc] for dx, dy, dc in order_g(side)]
    peers_t = [lax.rem(me_t + d, T) for d in order_t(T)]

    barrier = pltpu.get_barrier_semaphore()
    for p in peers_t:
        pl.semaphore_signal(barrier, inc=1, device_id=(me_g, p), device_id_type=MESH)
    for p in peers_g:
        pl.semaphore_signal(barrier, inc=1, device_id=(p, me_t), device_id_type=MESH)

    wo_rows = wo_hbm.shape[0]
    wo_base = pl.multiple_of(par * 64, 64)
    loads = [
        pltpu.make_async_copy(src, dst, local_sem.at[i])
        for i, (src, dst) in enumerate([
            (hid_hbm, hid), (wq_hbm, wq), (pt_hbm, pt), (len_hbm, lens), (kv_hbm, kv),
            (wo_hbm, wo.at[pl.ds(wo_base, wo_rows)]),
        ])
    ]
    for load in loads:
        load.start()
    cp_hid, cp_wq, cp_pt, cp_len, cp_kv, cp_wo = loads

    zero_base = pl.multiple_of((1 - par) * wo_rows, 64)
    wo[pl.ds(zero_base, 64), :] = jnp.zeros((64, wo.shape[1]), BF16)

    cp_hid.wait()
    cp_wq.wait()
    qkv = jnp.dot(hid[...], wq[...], preferred_element_type=F32).astype(BF16)
    qsend[...] = qkv
    qall[me_g] = qkv
    qown[me_t] = qkv

    def send_g(k, src, dst, chunked):
        for p in peers_g:
            pltpu.make_async_remote_copy(
                src_ref=src.at[p] if chunked else src, dst_ref=dst.at[me_g],
                send_sem=send_sem.at[k], recv_sem=recv_sem.at[k],
                device_id=(p, me_t), device_id_type=MESH,
            ).start()

    def send_t(k, src, dst, chunked):
        for p in peers_t:
            pltpu.make_async_remote_copy(
                src_ref=src.at[p] if chunked else src, dst_ref=dst.at[me_t],
                send_sem=send_sem.at[k], recv_sem=recv_sem.at[k],
                device_id=(me_g, p), device_id_type=MESH,
            ).start()

    def wait(sems, k, dst):
        most = dst.at[pl.ds(0, dst.shape[0] - 1)]
        pltpu.make_async_copy(most, most, sems.at[k]).wait()

    pl.semaphore_wait(barrier, G - 1 + T - 1)
    send_g(0, qsend, qall, False)
    send_t(1, qsend, qown, False)

    cp_pt.wait()
    cp_len.wait()

    def find(first, count):
        slot = first + iota((count, R), 0)
        marks = jnp.zeros((count, R), jnp.int32)
        for j in range(max_pages):
            marks = jnp.where(pt[j : j + 1, :] == slot, j + 1, marks)
        return marks

    held = (find(me_g * ring, ring) > 0).astype(F32).astype(BF16)
    eye = (iota((R, R), 0) == iota((R, R), 1)).astype(F32).astype(BF16)
    owns = lax.dot_general(
        eye, held, (((1,), (1,)), ((), ())), preferred_element_type=F32
    ) > 0.5
    marks = find(me_g * ring + me_t * S, S)
    live_col = jnp.sum(
        jnp.where(marks > 0, lens[...] - (marks - 1) * page_len, 0), axis=1, keepdims=True
    )
    live8 = iota((S, page_len), 1) < live_col
    live = jnp.concatenate([live8.astype(F32)] * HEADS, axis=0) > 0.5

    wait(recv_sem, 0, qall)
    q_rows = jnp.concatenate([qall[g] for g in range(G)], axis=0)
    chosen = jnp.dot(held, q_rows, preferred_element_type=F32)
    for t in range(T):
        bsend[t] = chosen[t * S : (t + 1) * S, :].astype(BF16)
    brecv[me_t] = bsend[me_t]
    send_t(2, bsend, brecv, True)

    cp_kv.wait()
    wait(recv_sem, 2, brecv)

    rows = HEADS * S
    kdim = KV_HEADS * hd
    row_slot = lax.rem(iota((rows, page_len), 0), S)
    empty = jnp.zeros((S, hd), F32)
    lines = []
    for h in range(HEADS):
        line = brecv[h // 2].astype(F32)[:, (h % 2) * hd : (h % 2 + 1) * hd]
        lines.append([line if g == h // PER_KV else empty for g in range(KV_HEADS)])
    q = jnp.concatenate(
        [jnp.concatenate([line[g] for line in lines], axis=0) for g in range(KV_HEADS)], axis=1
    ).astype(BF16)
    scores = jnp.zeros((rows, page_len), F32)
    for s in range(0, S, 2):
        key = kv[s : s + 2, :, 0:kdim].reshape(2 * page_len, kdim)
        part = lax.dot_general(q, key, (((1,), (1,)), ((), ())), preferred_element_type=F32)
        scores = jnp.where(row_slot == s, part[:, :page_len], scores)
        scores = jnp.where(row_slot == s + 1, part[:, page_len:], scores)
    scores = scores * scale
    top = jnp.max(jnp.where(live, scores, NEG), axis=1, keepdims=True)
    prob = jnp.where(live, jnp.exp(scores - top), 0.0).astype(BF16).astype(F32)
    total = jnp.sum(prob, axis=1, keepdims=True)
    acc = jnp.zeros((rows, kdim), F32)
    for s in range(0, S, 2):
        value = kv[s : s + 2, :, kdim : 2 * kdim].reshape(2 * page_len, kdim)
        pair = jnp.concatenate([jnp.where(row_slot == s + k, prob, 0.0) for k in range(2)], axis=1)
        acc = acc + jnp.dot(pair.astype(BF16), value, preferred_element_type=F32)

    lane = lax.rem(iota((rows, hd), 1), hd // 2)
    both = jnp.where(lane < 3, top, total)
    high = both.astype(BF16).astype(F32)
    mid = (both - high).astype(BF16).astype(F32)
    kind = lax.rem(lane, 3)
    stats = jnp.where(kind == 0, high, jnp.where(kind == 1, mid, both - high - mid))
    lane8 = iota((S, hd), 1)
    cut = lambda h: slice(h * S, (h + 1) * S)
    head_sum = lambda h: acc[cut(h), (h // PER_KV) * hd : (h // PER_KV + 1) * hd]
    for t in range(T):
        h = (3 * t) // 2
        pair_stats = jnp.where(lane8 < hd // 2, stats[cut(h)], stats[cut(h + 1)])
        dsend[t] = jnp.concatenate(
            [head_sum(h), head_sum(h + 1), pair_stats], axis=1
        ).astype(BF16)
    drecv[me_t] = dsend[me_t]
    send_t(3, dsend, drecv, True)
    wait(recv_sem, 3, drecv)

    got = drecv[...].astype(F32).reshape(ring, 3 * hd)
    same = iota((ring, ring), 0) == iota((ring, ring), 1)
    peaks, weights = [], []
    for i in range(2):
        c = 2 * hd + (hd // 2) * i
        m_col = got[:, c : c + 1] + got[:, c + 1 : c + 2] + got[:, c + 2 : c + 3]
        m_row = jnp.sum(jnp.where(same, m_col, 0.0), axis=0, keepdims=True)
        peak = jnp.max(jnp.where(owns, m_row, NEG), axis=1, keepdims=True)
        weight = jnp.exp(jnp.where(owns, m_row - peak, NEG))
        peaks.append(peak)
        high = weight.astype(BF16).astype(F32)
        weights += [high, weight - high]
    mixed = jnp.dot(
        jnp.concatenate(weights, axis=0).astype(BF16), got.astype(BF16),
        preferred_element_type=F32,
    )
    wholes, outs = [], []
    for i in range(2):
        both = mixed[2 * i * R : (2 * i + 1) * R] + mixed[(2 * i + 1) * R : (2 * i + 2) * R]
        c = 2 * hd + (hd // 2) * i + 3
        wholes.append(both[:, c : c + 1] + both[:, c + 1 : c + 2] + both[:, c + 2 : c + 3])
        outs.append(both[:, i * hd : (i + 1) * hd])
    mixed_stats = spread(peaks + wholes, iota((R, hd), 1), hd)
    packed = jnp.concatenate(outs + [mixed_stats], axis=1)
    per = R // G
    for g in range(G):
        esend[g] = packed[g * per : (g + 1) * per, :]
    erecv[me_g] = esend[me_g]
    send_g(4, esend, erecv, True)

    wait(recv_sem, 1, qown)
    first = lax.div(3 * me_t, 2)

    def own_head(h):
        pair = qown[lax.div(h, 2)].astype(F32)
        return jnp.where(lax.rem(h, 2) == 0, pair[:, :hd], pair[:, hd:])

    def own_kv(row, h):
        pair = qown[row].astype(F32)
        return jnp.where(lax.div(h, PER_KV) == 0, pair[:, :hd], pair[:, hd:])

    own_scores = [
        jnp.sum(own_head(first + i) * own_kv(6, first + i), axis=1, keepdims=True) * scale
        for i in range(2)
    ]
    own_values = [own_kv(7, first + i) for i in range(2)]
    cp_wo.wait()
    wait(recv_sem, 4, erecv)

    every = erecv[...]
    heads = []
    for i in range(2):
        m = every[:, :, 2 * hd + i : 2 * hd + i + 1]
        l = every[:, :, 2 * hd + 2 + i : 2 * hd + 3 + i]
        peak = jnp.maximum(jnp.max(m, axis=0), own_scores[i])
        f = jnp.exp(m - peak[None])
        own_f = jnp.exp(own_scores[i] - peak)
        whole = jnp.sum(f * l, axis=0) + own_f
        summed = jnp.sum(f * every[:, :, i * hd : (i + 1) * hd], axis=0) + own_f * own_values[i]
        heads.append(summed / whole)
    attn = jnp.concatenate(heads, axis=1)
    col = iota(attn.shape, 1)
    attn = jnp.where((col >= par * 64) & (col < par * 64 + wo_rows), attn, 0.0).astype(BF16)
    part = jnp.dot(attn, wo[...], preferred_element_type=F32)
    width = precv.shape[2]
    for t in range(T):
        psend[t] = part[:, t * width : (t + 1) * width]
    send_t(5, psend, precv, True)
    cp_own = pltpu.make_async_copy(psend.at[me_t], precv.at[me_t], local_sem.at[6])
    cp_own.start()
    wait(recv_sem, 5, precv)
    cp_own.wait()

    for k, dst in enumerate([qall, qown, brecv, drecv, erecv, precv]):
        wait(send_sem, k, dst)


def solution(mesh):
    G, T = mesh.shape["group"], mesh.shape["tp"]

    def on_device(hidden_in, w_qkv, w_out, kv_pool, page_table, lengths):
        per = hidden_in.shape[0]
        cols = w_qkv.shape[1]
        slots = kv_pool.shape[0]
        depth = w_out.shape[1]
        width = depth // T
        wide = 3 * HEAD_DIM
        dma = pltpu.SemaphoreType.DMA
        vm = pl.BlockSpec(memory_space=pltpu.VMEM)
        hbm = pl.BlockSpec(memory_space=pl.ANY)
        parts = pl.pallas_call(
            functools.partial(kernel, G, T),
            name="decode",
            out_shape=jax.ShapeDtypeStruct((T, per, width), F32),
            in_specs=[hbm] * 6,
            out_specs=hbm,
            scratch_shapes=[
                pltpu.VMEM(hidden_in.shape, BF16),
                pltpu.VMEM(page_table.shape[::-1], jnp.int32),
                pltpu.VMEM((1, lengths.shape[0]), jnp.int32),
                pltpu.VMEM(w_qkv.shape, BF16),
                pltpu.VMEM((2 * HEAD_DIM, depth), BF16),
                pltpu.VMEM(kv_pool.shape, BF16),
                pltpu.VMEM((per, cols), BF16),
                pltpu.VMEM((G, per, cols), BF16),
                pltpu.VMEM((T, per, cols), BF16),
                pltpu.VMEM((T, slots, cols), BF16),
                pltpu.VMEM((T, slots, cols), BF16),
                pltpu.VMEM((T, slots, wide), BF16),
                pltpu.VMEM((T, slots, wide), BF16),
                pltpu.VMEM((G, per, wide), F32),
                pltpu.VMEM((G, per, wide), F32),
                pltpu.VMEM((T, per, width), F32),
                dma((7,)), dma((6,)), dma((6,)),
            ],
            compiler_params=pltpu.CompilerParams(collective_id=0, has_side_effects=True),
        )(hidden_in, w_qkv, w_out, kv_pool, page_table.T, lengths.reshape(1, -1))
        return jnp.sum(parts, axis=0).astype(BF16)

    return jax.shard_map(
        on_device,
        mesh=mesh,
        in_specs=(
            P("group", None),
            P(None, "tp"),
            P("tp", None),
            P(("group", "tp"), None, None),
            P(),
            P(),
        ),
        out_specs=P("group", "tp"),
        check_vma=False,
    )
```

```python
import functools

import jax
import jax.numpy as jnp
from jax import lax
from jax.experimental import pallas as pl
from jax.experimental.pallas import tpu as pltpu
from jax.sharding import PartitionSpec as P

HEADS = 12
KV_HEADS = 2
HEAD_DIM = 128
PER_KV = HEADS // KV_HEADS
NEG = -1e30
MESH = pl.DeviceIdType.MESH
F32 = jnp.float32
BF16 = jnp.bfloat16


def iota(shape, dim):
    return lax.broadcasted_iota(jnp.int32, shape, dim)


def order_t(T):
    return sorted(range(1, T), key=lambda d: -min(d, T - d))


def order_g(n):
    hops = lambda d: min(d, n - d)
    all_d = [(x, y, c) for x in range(n) for y in range(n) for c in range(2)]
    return sorted(all_d[1:], key=lambda o: -(hops(o[0]) + hops(o[1])) * 2 - o[2])


def spread(columns, lane, width):
    out = columns[-1]
    for i in range(len(columns) - 2, -1, -1):
        out = jnp.where(lane == i, columns[i], out)
    return jnp.broadcast_to(out, (out.shape[0], width))


def kernel(
    G, T,
    hid_hbm, wq_hbm, wo_hbm, kv_hbm, pt_hbm, len_hbm, precv,
    hid, pt, lens, wq, wo, kv,
    qsend, qall, qown, bsend, brecv, dsend, drecv, esend, erecv, psend,
    local_sem, send_sem, recv_sem,
):
    me_g = lax.axis_index("group")
    me_t = lax.axis_index("tp")
    scale = HEAD_DIM ** (-0.5)
    S = kv_hbm.shape[0]
    page_len = kv_hbm.shape[1]
    max_pages, R = pt_hbm.shape
    ring = S * T
    par = lax.rem(me_t, 2)
    hd = HEAD_DIM
    side = 1
    while 2 * side * side < G:
        side += 1

    xs = [lax.rem(lax.div(me_g, 2 * side) + d, side) * (2 * side) for d in range(side)]
    ys = [lax.rem(lax.rem(lax.div(me_g, 2), side) + d, side) * 2 for d in range(side)]
    cs = [lax.rem(lax.rem(me_g, 2) + d, 2) for d in range(2)]
    peers_g = [xs[dx] + ys[dy] + cs[dc] for dx, dy, dc in order_g(side)]
    peers_t = [lax.rem(me_t + d, T) for d in order_t(T)]

    barrier = pltpu.get_barrier_semaphore()
    for p in peers_t:
        pl.semaphore_signal(barrier, inc=1, device_id=(me_g, p), device_id_type=MESH)
    for p in peers_g:
        pl.semaphore_signal(barrier, inc=1, device_id=(p, me_t), device_id_type=MESH)

    wo_rows = wo_hbm.shape[0]
    wo_base = pl.multiple_of(par * 64, 64)
    loads = [
        pltpu.make_async_copy(src, dst, local_sem.at[i])
        for i, (src, dst) in enumerate([
            (hid_hbm, hid), (wq_hbm, wq), (pt_hbm, pt), (len_hbm, lens), (kv_hbm, kv),
            (wo_hbm, wo.at[pl.ds(wo_base, wo_rows)]),
        ])
    ]
    for load in loads:
        load.start()
    cp_hid, cp_wq, cp_pt, cp_len, cp_kv, cp_wo = loads

    zero_base = pl.multiple_of((1 - par) * wo_rows, 64)
    wo[pl.ds(zero_base, 64), :] = jnp.zeros((64, wo.shape[1]), BF16)

    cp_hid.wait()
    cp_wq.wait()
    qkv = jnp.dot(hid[...], wq[...], preferred_element_type=F32).astype(BF16)
    qsend[...] = qkv
    qall[me_g] = qkv
    qown[me_t] = qkv

    def send_g(k, src, dst, chunked):
        for p in peers_g:
            pltpu.make_async_remote_copy(
                src_ref=src.at[p] if chunked else src, dst_ref=dst.at[me_g],
                send_sem=send_sem.at[k], recv_sem=recv_sem.at[k],
                device_id=(p, me_t), device_id_type=MESH,
            ).start()

    def copy_t(k, src, dst, p):
        return pltpu.make_async_remote_copy(
            src_ref=src, dst_ref=dst.at[me_t],
            send_sem=send_sem.at[k], recv_sem=recv_sem.at[k],
            device_id=(me_g, p), device_id_type=MESH,
        )

    def send_t(k, src, dst, chunked):
        for p in peers_t:
            copy_t(k, src.at[p] if chunked else src, dst, p).start()

    def wait(sems, k, dst):
        most = dst.at[pl.ds(0, dst.shape[0] - 1)]
        pltpu.make_async_copy(most, most, sems.at[k]).wait()

    pl.semaphore_wait(barrier, G - 1 + T - 1)
    send_g(0, qsend, qall, False)
    send_t(1, qsend, qown, False)

    cp_pt.wait()
    cp_len.wait()

    def find(first, count):
        slot = first + iota((count, R), 0)
        marks = jnp.zeros((count, R), jnp.int32)
        for j in range(max_pages):
            marks = jnp.where(pt[j : j + 1, :] == slot, j + 1, marks)
        return marks

    held = (find(me_g * ring, ring) > 0).astype(F32).astype(BF16)
    eye = (iota((R, R), 0) == iota((R, R), 1)).astype(F32).astype(BF16)
    owns = lax.dot_general(
        eye, jnp.concatenate([held, held], axis=0), (((1,), (1,)), ((), ())),
        preferred_element_type=F32,
    ) > 0.5
    marks = find(me_g * ring + me_t * S, S)
    live_col = jnp.sum(
        jnp.where(marks > 0, lens[...] - (marks - 1) * page_len, 0), axis=1, keepdims=True
    )
    live8 = iota((S, page_len), 1) < live_col
    live = jnp.concatenate([live8.astype(F32)] * HEADS, axis=0) > 0.5

    wait(recv_sem, 0, qall)
    q_rows = jnp.concatenate([qall[g] for g in range(G)], axis=0)
    chosen = jnp.dot(held, q_rows, preferred_element_type=F32)
    for t in range(T):
        bsend[t] = chosen[t * S : (t + 1) * S, :].astype(BF16)
    brecv[me_t] = bsend[me_t]
    send_t(2, bsend, brecv, True)

    cp_kv.wait()
    wait(recv_sem, 2, brecv)

    rows = HEADS * S
    kdim = KV_HEADS * hd
    row_slot = lax.rem(iota((rows, page_len), 0), S)
    empty = jnp.zeros((S, hd), F32)
    lines = []
    for h in range(HEADS):
        line = brecv[h // 2].astype(F32)[:, (h % 2) * hd : (h % 2 + 1) * hd]
        lines.append([line if g == h // PER_KV else empty for g in range(KV_HEADS)])
    q = jnp.concatenate(
        [jnp.concatenate([line[g] for line in lines], axis=0) for g in range(KV_HEADS)], axis=1
    ).astype(BF16)
    scores = jnp.zeros((rows, page_len), F32)
    for s in range(0, S, 2):
        key = kv[s : s + 2, :, 0:kdim].reshape(2 * page_len, kdim)
        part = lax.dot_general(q, key, (((1,), (1,)), ((), ())), preferred_element_type=F32)
        scores = jnp.where(row_slot == s, part[:, :page_len], scores)
        scores = jnp.where(row_slot == s + 1, part[:, page_len:], scores)
    scores = scores * scale
    top = jnp.max(jnp.where(live, scores, NEG), axis=1, keepdims=True)
    prob = jnp.where(live, jnp.exp(scores - top), 0.0).astype(BF16).astype(F32)
    total = jnp.sum(prob, axis=1, keepdims=True)
    acc = jnp.zeros((rows, kdim), F32)
    for s in range(0, S, 2):
        value = kv[s : s + 2, :, kdim : 2 * kdim].reshape(2 * page_len, kdim)
        pair = jnp.concatenate([jnp.where(row_slot == s + k, prob, 0.0) for k in range(2)], axis=1)
        acc = acc + jnp.dot(pair.astype(BF16), value, preferred_element_type=F32)

    lane = lax.rem(iota((rows, hd), 1), hd // 2)
    both = jnp.where(lane < 3, top, total)
    high = both.astype(BF16).astype(F32)
    mid = (both - high).astype(BF16).astype(F32)
    kind = lax.rem(lane, 3)
    stats = jnp.where(kind == 0, high, jnp.where(kind == 1, mid, both - high - mid))
    lane8 = iota((S, hd), 1)
    cut = lambda h: slice(h * S, (h + 1) * S)
    head_sum = lambda h: acc[cut(h), (h // PER_KV) * hd : (h // PER_KV + 1) * hd]
    for t in range(T):
        h = (3 * t) // 2
        pair_stats = jnp.where(lane8 < hd // 2, stats[cut(h)], stats[cut(h + 1)])
        dsend[t] = jnp.concatenate(
            [head_sum(h), head_sum(h + 1), pair_stats], axis=1
        ).astype(BF16)
    drecv[me_t] = dsend[me_t]
    send_t(3, dsend, drecv, True)
    wait(recv_sem, 3, drecv)

    got = drecv[...].astype(F32).reshape(ring, 3 * hd)
    stats = got[:, 2 * hd : 3 * hd]
    half = iota((R, 2 * ring), 1) < ring
    same = iota((ring, 2 * ring), 0) == lax.rem(iota((ring, 2 * ring), 1), ring)
    peaks, wholes, outs = [], [], []
    for i in range(2):
        c = (hd // 2) * i
        m_col = stats[:, c : c + 1] + stats[:, c + 1 : c + 2] + stats[:, c + 2 : c + 3]
        m_row = jnp.sum(jnp.where(same, m_col, 0.0), axis=0, keepdims=True)
        peak = jnp.max(jnp.where(owns, m_row, NEG), axis=1, keepdims=True)
        weight = jnp.exp(jnp.where(owns, m_row - peak, NEG))
        high = weight.astype(BF16).astype(F32)
        weight = jnp.where(half, high, weight - high).astype(BF16)
        block = jnp.concatenate([got[:, i * hd : (i + 1) * hd], stats], axis=1).astype(BF16)
        mixed = jnp.dot(
            weight, jnp.concatenate([block, block], axis=0), preferred_element_type=F32
        )
        c = hd + (hd // 2) * i + 3
        peaks.append(peak)
        wholes.append(mixed[:, c : c + 1] + mixed[:, c + 1 : c + 2] + mixed[:, c + 2 : c + 3])
        outs.append(mixed[:, :hd])
    mixed_stats = spread(peaks + wholes, iota((R, hd), 1), hd)
    packed = jnp.concatenate(outs + [mixed_stats], axis=1)
    per = R // G
    for g in range(G):
        esend[g] = packed[g * per : (g + 1) * per, :]
    erecv[me_g] = esend[me_g]
    send_g(4, esend, erecv, True)

    wait(recv_sem, 1, qown)
    first = lax.div(3 * me_t, 2)

    def own_head(h):
        pair = qown[lax.div(h, 2)].astype(F32)
        return jnp.where(lax.rem(h, 2) == 0, pair[:, :hd], pair[:, hd:])

    def own_kv(row, h):
        pair = qown[row].astype(F32)
        return jnp.where(lax.div(h, PER_KV) == 0, pair[:, :hd], pair[:, hd:])

    own_scores = [
        jnp.sum(own_head(first + i) * own_kv(6, first + i), axis=1, keepdims=True) * scale
        for i in range(2)
    ]
    own_values = [own_kv(7, first + i) for i in range(2)]
    cp_wo.wait()
    wait(recv_sem, 4, erecv)

    every = erecv[...]
    heads = []
    for i in range(2):
        m = every[:, :, 2 * hd + i : 2 * hd + i + 1]
        l = every[:, :, 2 * hd + 2 + i : 2 * hd + 3 + i]
        peak = jnp.maximum(jnp.max(m, axis=0), own_scores[i])
        f = jnp.exp(m - peak[None])
        own_f = jnp.exp(own_scores[i] - peak)
        whole = jnp.sum(f * l, axis=0) + own_f
        summed = jnp.sum(f * every[:, :, i * hd : (i + 1) * hd], axis=0) + own_f * own_values[i]
        heads.append(summed / whole)
    attn = jnp.concatenate(heads, axis=1)
    col = iota(attn.shape, 1)
    attn = jnp.where((col >= par * 64) & (col < par * 64 + wo_rows), attn, 0.0).astype(BF16)
    width = precv.shape[2]
    for p in peers_t + [me_t]:
        columns = pl.ds(pl.multiple_of(p * width, width), width)
        psend[p] = jnp.dot(attn, wo[:, columns], preferred_element_type=F32)
        if p is not me_t:
            copy_t(5, psend.at[p], precv, p).start()
    cp_own = pltpu.make_async_copy(psend.at[me_t], precv.at[me_t], local_sem.at[6])
    cp_own.start()
    wait(recv_sem, 5, precv)
    cp_own.wait()

    for k, dst in enumerate([qall, qown, brecv, drecv, erecv, precv]):
        wait(send_sem, k, dst)


def solution(mesh):
    G, T = mesh.shape["group"], mesh.shape["tp"]

    def on_device(hidden_in, w_qkv, w_out, kv_pool, page_table, lengths):
        per = hidden_in.shape[0]
        cols = w_qkv.shape[1]
        slots = kv_pool.shape[0]
        depth = w_out.shape[1]
        width = depth // T
        wide = 3 * HEAD_DIM
        dma = pltpu.SemaphoreType.DMA
        vm = pl.BlockSpec(memory_space=pltpu.VMEM)
        hbm = pl.BlockSpec(memory_space=pl.ANY)
        parts = pl.pallas_call(
            functools.partial(kernel, G, T),
            name="decode",
            out_shape=jax.ShapeDtypeStruct((T, per, width), F32),
            in_specs=[pl.BlockSpec(memory_space=pltpu.HBM)] * 6,
            out_specs=hbm,
            scratch_shapes=[
                pltpu.VMEM(hidden_in.shape, BF16),
                pltpu.VMEM(page_table.shape[::-1], jnp.int32),
                pltpu.VMEM((1, lengths.shape[0]), jnp.int32),
                pltpu.VMEM(w_qkv.shape, BF16),
                pltpu.VMEM((2 * HEAD_DIM, depth), BF16),
                pltpu.VMEM(kv_pool.shape, BF16),
                pltpu.VMEM((per, cols), BF16),
                pltpu.VMEM((G, per, cols), BF16),
                pltpu.VMEM((T, per, cols), BF16),
                pltpu.VMEM((T, slots, cols), BF16),
                pltpu.VMEM((T, slots, cols), BF16),
                pltpu.VMEM((T, slots, wide), BF16),
                pltpu.VMEM((T, slots, wide), BF16),
                pltpu.VMEM((G, per, wide), F32),
                pltpu.VMEM((G, per, wide), F32),
                pltpu.VMEM((T, per, width), F32),
                dma((7,)), dma((6,)), dma((6,)),
            ],
            compiler_params=pltpu.CompilerParams(collective_id=0, has_side_effects=True, vmem_limit_bytes=12 * 2**20),
        )(*[pltpu.with_memory_space_constraint(x, pltpu.HBM) for x in (hidden_in, w_qkv, w_out, kv_pool, page_table.T, lengths.reshape(1, -1))])
        return jnp.sum(parts, axis=0).astype(BF16)

    return jax.shard_map(
        on_device,
        mesh=mesh,
        in_specs=(
            P("group", None),
            P(None, "tp"),
            P("tp", None),
            P(("group", "tp"), None, None),
            P(),
            P(),
        ),
        out_specs=P("group", "tp"),
        check_vma=False,
    )
```

```python
import functools

import jax
import jax.numpy as jnp
from jax import lax
from jax.experimental import pallas as pl
from jax.experimental.pallas import tpu as pltpu
from jax.sharding import PartitionSpec as P

HEADS = 12
KV_HEADS = 2
HEAD_DIM = 128
PER_KV = HEADS // KV_HEADS
NEG = -1e30
MESH = pl.DeviceIdType.MESH
F32 = jnp.float32
BF16 = jnp.bfloat16


def iota(shape, dim):
    return lax.broadcasted_iota(jnp.int32, shape, dim)


def order_t(T):
    return sorted(range(1, T), key=lambda d: -min(d, T - d))


def order_g(n):
    hops = lambda d: min(d, n - d)
    all_d = [(x, y, c) for x in range(n) for y in range(n) for c in range(2)]
    return sorted(all_d[1:], key=lambda o: -(hops(o[0]) + hops(o[1])) * 2 - o[2])


def kernel(
    G, T,
    hid_hbm, wq_hbm, wo_hbm, kv_hbm, pt_hbm, len_hbm, precv,
    hid, pt, lens, wq, wo, kv,
    qsend, qall, qown, bsend, brecv, dsend, drecv, esend, erecv, psend,
    local_sem, send_sem, recv_sem,
):
    me_g = lax.axis_index("group")
    me_t = lax.axis_index("tp")
    scale = HEAD_DIM ** (-0.5)
    S = kv_hbm.shape[0]
    page_len = kv_hbm.shape[1]
    max_pages, R = pt_hbm.shape
    ring = S * T
    par = lax.rem(me_t, 2)
    hd = HEAD_DIM
    side = 1
    while 2 * side * side < G:
        side += 1

    xs = [lax.rem(lax.div(me_g, 2 * side) + d, side) * (2 * side) for d in range(side)]
    ys = [lax.rem(lax.rem(lax.div(me_g, 2), side) + d, side) * 2 for d in range(side)]
    cs = [lax.rem(lax.rem(me_g, 2) + d, 2) for d in range(2)]
    peers_g = [xs[dx] + ys[dy] + cs[dc] for dx, dy, dc in order_g(side)]
    peers_t = [lax.rem(me_t + d, T) for d in order_t(T)]

    barrier = pltpu.get_barrier_semaphore()
    for p in peers_g:
        pl.semaphore_signal(barrier, inc=1, device_id=(p, me_t), device_id_type=MESH)
    for p in peers_t:
        pl.semaphore_signal(barrier, inc=1, device_id=(me_g, p), device_id_type=MESH)

    wo_rows = wo_hbm.shape[0]
    wo_base = pl.multiple_of(par * 64, 64)
    loads = [
        pltpu.make_async_copy(src, dst, local_sem.at[i])
        for i, (src, dst) in enumerate([
            (hid_hbm, hid), (wq_hbm, wq), (pt_hbm, pt), (len_hbm, lens), (kv_hbm, kv),
            (wo_hbm, wo.at[pl.ds(wo_base, wo_rows)]),
        ])
    ]
    for load in loads:
        load.start()
    cp_hid, cp_wq, cp_pt, cp_len, cp_kv, cp_wo = loads

    zero_base = pl.multiple_of((1 - par) * wo_rows, 64)
    wo[pl.ds(zero_base, 64), :] = jnp.zeros((64, wo.shape[1]), BF16)

    cp_hid.wait()
    cp_wq.wait()
    qkv = jnp.dot(hid[...], wq[...], preferred_element_type=F32).astype(BF16)
    qsend[...] = qkv
    qall[me_g] = qkv
    qown[me_t] = qkv

    def send_g(k, src, dst, chunked):
        for p in peers_g:
            pltpu.make_async_remote_copy(
                src_ref=src.at[p] if chunked else src, dst_ref=dst.at[me_g],
                send_sem=send_sem.at[k], recv_sem=recv_sem.at[k],
                device_id=(p, me_t), device_id_type=MESH,
            ).start()

    def copy_t(k, src, dst, p):
        return pltpu.make_async_remote_copy(
            src_ref=src, dst_ref=dst.at[me_t],
            send_sem=send_sem.at[k], recv_sem=recv_sem.at[k],
            device_id=(me_g, p), device_id_type=MESH,
        )

    def send_t(k, src, dst, chunked):
        for p in peers_t:
            copy_t(k, src.at[p] if chunked else src, dst, p).start()

    def wait(sems, k, dst):
        most = dst.at[pl.ds(0, dst.shape[0] - 1)]
        pltpu.make_async_copy(most, most, sems.at[k]).wait()

    pl.semaphore_wait(barrier, G - 1 + T - 1)
    send_g(0, qsend, qall, False)
    send_t(1, qsend, qown, False)

    cp_pt.wait()
    cp_len.wait()

    def find(first, count):
        slot = first + iota((count, R), 0)
        marks = jnp.zeros((count, R), jnp.int32)
        for j in range(max_pages):
            marks = jnp.where(pt[j : j + 1, :] == slot, j + 1, marks)
        return marks

    held = (find(me_g * ring, ring) > 0).astype(F32).astype(BF16)
    eye = (iota((R, R), 0) == iota((R, R), 1)).astype(F32).astype(BF16)
    owns = lax.dot_general(
        eye, jnp.concatenate([held, held], axis=0), (((1,), (1,)), ((), ())),
        preferred_element_type=F32,
    ) > 0.5
    marks = find(me_g * ring + me_t * S, S)
    live_col = jnp.sum(
        jnp.where(marks > 0, lens[...] - (marks - 1) * page_len, 0), axis=1, keepdims=True
    )
    live8 = iota((S, page_len), 1) < live_col
    live = jnp.concatenate([live8.astype(F32)] * HEADS, axis=0) > 0.5

    wait(recv_sem, 0, qall)
    q_rows = jnp.concatenate([qall[g] for g in range(G)], axis=0)
    chosen = jnp.dot(held, q_rows, preferred_element_type=F32)
    for t in range(T):
        bsend[t] = chosen[t * S : (t + 1) * S, :].astype(BF16)
    brecv[me_t] = bsend[me_t]
    send_t(2, bsend, brecv, True)

    cp_kv.wait()
    wait(recv_sem, 2, brecv)

    rows = HEADS * S
    kdim = KV_HEADS * hd
    row_slot = lax.rem(iota((rows, page_len), 0), S)
    empty = jnp.zeros((S, hd), F32)
    lines = []
    for h in range(HEADS):
        line = brecv[h // 2].astype(F32)[:, (h % 2) * hd : (h % 2 + 1) * hd]
        lines.append([line if g == h // PER_KV else empty for g in range(KV_HEADS)])
    q = jnp.concatenate(
        [jnp.concatenate([line[g] for line in lines], axis=0) for g in range(KV_HEADS)], axis=1
    ).astype(BF16)
    scores = jnp.zeros((rows, page_len), F32)
    for s in range(0, S, 2):
        key = kv[s : s + 2, :, 0:kdim].reshape(2 * page_len, kdim)
        part = lax.dot_general(q, key, (((1,), (1,)), ((), ())), preferred_element_type=F32)
        scores = jnp.where(row_slot == s, part[:, :page_len], scores)
        scores = jnp.where(row_slot == s + 1, part[:, page_len:], scores)
    scores = scores * scale
    top = jnp.max(jnp.where(live, scores, NEG), axis=1, keepdims=True)
    prob = jnp.where(live, jnp.exp(scores - top), 0.0).astype(BF16).astype(F32)
    total = jnp.sum(prob, axis=1, keepdims=True)
    acc = jnp.zeros((rows, kdim), F32)
    for s in range(0, S, 2):
        value = kv[s : s + 2, :, kdim : 2 * kdim].reshape(2 * page_len, kdim)
        pair = jnp.concatenate([jnp.where(row_slot == s + k, prob, 0.0) for k in range(2)], axis=1)
        acc = acc + jnp.dot(pair.astype(BF16), value, preferred_element_type=F32)

    lane = lax.rem(iota((rows, hd), 1), hd // 2)
    both = jnp.where(lane < 3, top, total)
    high = both.astype(BF16).astype(F32)
    mid = (both - high).astype(BF16).astype(F32)
    kind = lax.rem(lane, 3)
    stats = jnp.where(kind == 0, high, jnp.where(kind == 1, mid, both - high - mid))
    lane8 = iota((S, hd), 1)
    cut = lambda h: slice(h * S, (h + 1) * S)
    head_sum = lambda h: acc[cut(h), (h // PER_KV) * hd : (h // PER_KV + 1) * hd]
    for t in range(T):
        h = (3 * t) // 2
        pair_stats = jnp.where(lane8 < hd // 2, stats[cut(h)], stats[cut(h + 1)])
        dsend[t] = jnp.concatenate(
            [head_sum(h), head_sum(h + 1), pair_stats], axis=1
        ).astype(BF16)
    drecv[me_t] = dsend[me_t]
    send_t(3, dsend, drecv, True)
    wait(recv_sem, 3, drecv)

    got = drecv[...].astype(F32).reshape(ring, 3 * hd)
    stats = got[:, 2 * hd : 3 * hd]
    half = iota((R, 2 * ring), 1) < ring
    same = iota((ring, 2 * ring), 0) == lax.rem(iota((ring, 2 * ring), 1), ring)
    peaks, wholes, outs = [], [], []
    for i in range(2):
        c = (hd // 2) * i
        m_col = stats[:, c : c + 1] + stats[:, c + 1 : c + 2] + stats[:, c + 2 : c + 3]
        m_row = jnp.sum(jnp.where(same, m_col, 0.0), axis=0, keepdims=True)
        peak = jnp.max(jnp.where(owns, m_row, NEG), axis=1, keepdims=True)
        weight = jnp.exp(jnp.where(owns, m_row - peak, NEG))
        high = weight.astype(BF16).astype(F32)
        weight = jnp.where(half, high, weight - high).astype(BF16)
        block = jnp.concatenate([got[:, i * hd : (i + 1) * hd], stats], axis=1).astype(BF16)
        mixed = jnp.dot(
            weight, jnp.concatenate([block, block], axis=0), preferred_element_type=F32
        )
        c = hd + (hd // 2) * i + 3
        peaks.append(peak)
        wholes.append(mixed[:, c : c + 1] + mixed[:, c + 1 : c + 2] + mixed[:, c + 2 : c + 3])
        outs.append(mixed[:, :hd])
    even = lax.rem(iota((R, hd), 1), 2) == 0
    packed = jnp.concatenate(
        outs + [jnp.where(even, peaks[0], peaks[1]), jnp.where(even, wholes[0], wholes[1])],
        axis=1,
    )
    per = R // G
    for g in range(G):
        esend[g] = packed[g * per : (g + 1) * per, :]
    erecv[me_g] = esend[me_g]
    send_g(4, esend, erecv, True)

    wait(recv_sem, 1, qown)
    first = lax.div(3 * me_t, 2)

    def own_head(h):
        pair = qown[lax.div(h, 2)].astype(F32)
        return jnp.where(lax.rem(h, 2) == 0, pair[:, :hd], pair[:, hd:])

    def own_kv(row, h):
        pair = qown[row].astype(F32)
        return jnp.where(lax.div(h, PER_KV) == 0, pair[:, :hd], pair[:, hd:])

    own_scores = [
        jnp.sum(own_head(first + i) * own_kv(6, first + i), axis=1, keepdims=True) * scale
        for i in range(2)
    ]
    pick = lax.rem(iota((per, hd), 1), 2) == 0
    own_score = jnp.where(pick, own_scores[0], own_scores[1])
    own_values = [own_kv(7, first + i) for i in range(2)]
    cp_wo.wait()
    wait(recv_sem, 4, erecv)

    m = erecv[:, :, 2 * hd : 3 * hd]
    peak = jnp.maximum(jnp.max(m, axis=0), own_score)
    f = jnp.exp(m - peak[None])
    own_f = jnp.exp(own_score - peak)
    whole = jnp.sum(f * erecv[:, :, 3 * hd : 4 * hd], axis=0) + own_f
    heads = []
    for i in range(2):
        summed = jnp.sum(f[:, :, i : i + 1] * erecv[:, :, i * hd : (i + 1) * hd], axis=0)
        heads.append((summed + own_f[:, i : i + 1] * own_values[i]) / whole[:, i : i + 1])
    attn = jnp.concatenate(heads, axis=1)
    col = iota(attn.shape, 1)
    attn = jnp.where((col >= par * 64) & (col < par * 64 + wo_rows), attn, 0.0).astype(BF16)
    width = precv.shape[2]
    for p in peers_t + [me_t]:
        columns = pl.ds(pl.multiple_of(p * width, width), width)
        psend[p] = jnp.dot(attn, wo[:, columns], preferred_element_type=F32)
        if p is not me_t:
            copy_t(5, psend.at[p], precv, p).start()
    cp_own = pltpu.make_async_copy(psend.at[me_t], precv.at[me_t], local_sem.at[6])
    cp_own.start()
    wait(recv_sem, 5, precv)
    cp_own.wait()

    for k, dst in enumerate([qall, qown, brecv, drecv, erecv, precv]):
        wait(send_sem, k, dst)


def solution(mesh):
    G, T = mesh.shape["group"], mesh.shape["tp"]

    def on_device(hidden_in, w_qkv, w_out, kv_pool, page_table, lengths):
        per = hidden_in.shape[0]
        cols = w_qkv.shape[1]
        slots = kv_pool.shape[0]
        depth = w_out.shape[1]
        width = depth // T
        wide = 3 * HEAD_DIM
        dma = pltpu.SemaphoreType.DMA
        vm = pl.BlockSpec(memory_space=pltpu.VMEM)
        hbm = pl.BlockSpec(memory_space=pl.ANY)
        parts = pl.pallas_call(
            functools.partial(kernel, G, T),
            name="decode",
            out_shape=jax.ShapeDtypeStruct((T, per, width), F32),
            in_specs=[pl.BlockSpec(memory_space=pltpu.HBM)] * 6,
            out_specs=hbm,
            scratch_shapes=[
                pltpu.VMEM(hidden_in.shape, BF16),
                pltpu.VMEM(page_table.shape[::-1], jnp.int32),
                pltpu.VMEM((1, lengths.shape[0]), jnp.int32),
                pltpu.VMEM(w_qkv.shape, BF16),
                pltpu.VMEM((2 * HEAD_DIM, depth), BF16),
                pltpu.VMEM(kv_pool.shape, BF16),
                pltpu.VMEM((per, cols), BF16),
                pltpu.VMEM((G, per, cols), BF16),
                pltpu.VMEM((T, per, cols), BF16),
                pltpu.VMEM((T, slots, cols), BF16),
                pltpu.VMEM((T, slots, cols), BF16),
                pltpu.VMEM((T, slots, wide), BF16),
                pltpu.VMEM((T, slots, wide), BF16),
                pltpu.VMEM((G, per, wide + HEAD_DIM), F32),
                pltpu.VMEM((G, per, wide + HEAD_DIM), F32),
                pltpu.VMEM((T, per, width), F32),
                dma((7,)), dma((6,)), dma((6,)),
            ],
            compiler_params=pltpu.CompilerParams(collective_id=0, has_side_effects=True, vmem_limit_bytes=12 * 2**20),
        )(*[pltpu.with_memory_space_constraint(x, pltpu.HBM) for x in (hidden_in, w_qkv, w_out, kv_pool, page_table.T, lengths.reshape(1, -1))])
        return jnp.sum(parts, axis=0).astype(BF16)

    return jax.shard_map(
        on_device,
        mesh=mesh,
        in_specs=(
            P("group", None),
            P(None, "tp"),
            P("tp", None),
            P(("group", "tp"), None, None),
            P(),
            P(),
        ),
        out_specs=P("group", "tp"),
        check_vma=False,
    )
```
